768 devices in a mesh: dp: 48 (over z, y_lo), fsdp: 16 (over x, y_hi, core).
Axes of the slice: x: 4, y: 8 (y_hi: 2, y_lo: 4; y = y_hi * 4 + y_lo), z: 12, core: 2. Of those that a mesh axis runs over, the one named last changes fastest.
Arguments:
- inputs: float32 [640, 49152], P('fsdp', 'dp'), may hold values from -26 to 26, as said below
- norm_gain: float32 [640], P('fsdp'), may hold values from 0.1 to 1.9
- norm_bias: float32 [640], P('fsdp'), may hold values from -3 to 3
- conv_weight: float32 [9, 640, 640], P(None, 'fsdp'), may hold values from -0.078125 to 0.078125
- moment_one: float32 [9, 640, 640], P(None, 'fsdp'), may hold values from -3 to 3
- moment_two: float32 [9, 640, 640], P(None, 'fsdp'), may hold values from 0.5 to 4
- out_grad: float32 [640, 49152], P('fsdp', 'dp'), may hold values from -6 to 6
Outputs:
- block_out: float32 [640, 49152], P('fsdp', 'dp')
- input_grad: float32 [640, 49152], P('fsdp', 'dp')
- new_weight: float32 [9, 640, 640], P(None, 'fsdp')
- new_moment_one: float32 [9, 640, 640], P(None, 'fsdp')
- new_moment_two: float32 [9, 640, 640], P(None, 'fsdp')
The draws below stay inside these ranges and needn't reach their ends.
Inputs may be any that keep to these rules, and one draw needn't show every extreme that they name: `inputs`: activations of mixed channel and pixel scales.
All inputs are finite; a program needn't handle non-finite values.
Results may differ from the reference program's by a relative error of at most 0.0027.
Values may be sent and summed in bfloat16 or wider, within the bound.
No kernel may reach another device: no remote copies, remote signals or barrier semaphores. Data moves between devices by JAX's collectives and lax.ppermute only.
A program may use at most 32 MiB of HBM per device.

```python
import math
import jax
import jax.numpy as jnp
from jax import lax

CHANNELS = 640
GROUP_CH = 40
SIDE = 32
IMG_GRP = 1
PIXELS = 49152
N_DP = 48


def draw_inputs(key, part):
    key_scale, key_pixel, key_base, key_offset = jax.random.split(key, 4)
    chan_scale = jnp.exp(jax.random.uniform(key_scale, (CHANNELS, 1), jnp.float32, math.log(0.3), math.log(3.0)))
    pixel_scale = jnp.exp(jax.random.uniform(key_pixel, (1, PIXELS), jnp.float32, math.log(0.5), math.log(2.0)))
    base = jnp.clip(jax.random.normal(key_base, (CHANNELS, PIXELS), jnp.float32), -4.0, 4.0)
    offset = jnp.clip(0.5 * jax.random.normal(key_offset, (CHANNELS, 1), jnp.float32), -1.5, 1.5)
    return (base * chan_scale * pixel_scale + offset).astype(jnp.float32)


def level_of(key, shape, pieces, smallest, top_value):
    gain = 1.0
    for axis_at, parts in pieces:
        heights = jax.random.uniform(jax.random.fold_in(jax.random.fold_in(key, 6), axis_at), (parts,), jnp.float32, smallest / len(pieces), top_value / len(pieces))
        gain = gain * jnp.repeat(jnp.exp(heights), shape[axis_at] // parts).reshape((-1,) + (1,) * (len(shape) - 1 - axis_at))
    return gain


def gaussian(own_key, extent, spread, reach, shards=(), kind=jnp.bfloat16):
    values = jax.random.normal(own_key, extent, jnp.float32) * spread
    if len(shards) > 0:
        values = level_of(own_key, extent, shards, -0.22, 0.18) * values
    return jnp.clip(values, min=-reach, max=reach).astype(kind)


def setup_inputs(seed: int = 0) -> dict:
    seeds = jax.random.split(jax.random.key(seed), 8)
    return {
        "inputs": draw_inputs(jax.random.fold_in(seeds[7], 71), 0),
        "norm_gain": jnp.clip(1.0 + 0.18 * jax.random.normal(seeds[1], (CHANNELS,), jnp.float32), 0.1, 1.9),
        "norm_bias": gaussian(seeds[2], (CHANNELS,), 0.5, 3.0, ((0, 16),), jnp.float32),
        "conv_weight": gaussian(seeds[3], (9, CHANNELS, CHANNELS), (9 * CHANNELS) ** -0.5, 0.078125, ((1, 16),), jnp.float32),
        "moment_one": gaussian(seeds[4], (9, CHANNELS, CHANNELS), 0.5, 3.0, ((1, 16),), jnp.float32),
        "moment_two": jnp.clip(jnp.exp(math.log(4.0) - 2.0794415 * jax.random.uniform(seeds[5], (9, CHANNELS, CHANNELS), jnp.float32) ** level_of(seeds[5], (9, CHANNELS, CHANNELS), ((1, 16),), -0.2, 0.2)), 0.5, 4.0),
        "out_grad": gaussian(seeds[6], (CHANNELS, PIXELS), 1.0, 6.0, ((0, 16), (1, 48)), jnp.float32),
    }


EPS_NORM = 1e-05
BETA_ONE = 0.9
BETA_TWO = 0.999
CORRECT_ONE = 1.0 - 0.9 ** 10
CORRECT_TWO = 1.0 - 0.999 ** 10
LEARN_RATE = 0.001
EPS_ADAM = 1e-08
OFFSETS = ((-1, -1), (-1, 0), (-1, 1), (0, -1), (0, 0), (0, 1), (1, -1), (1, 0), (1, 1))

def shifted(source, row_step, col_step):
    width_all = source.shape[-1]
    position = jnp.arange(width_all, dtype=jnp.int32)
    row_pos = position // SIDE % SIDE
    col_pos = position % SIDE
    inside = (row_pos + row_step >= 0) & (row_pos + row_step < SIDE) & (col_pos + col_step >= 0) & (col_pos + col_step < SIDE)
    margin = SIDE + 1
    padded = jnp.pad(source, ((0, 0), (margin, margin)))
    start_at = margin + row_step * SIDE + col_step
    moved = padded[:, start_at:start_at + width_all]
    return jnp.where(inside[None, :], moved, jnp.zeros_like(moved))

def group_stats(source, norm_gain, norm_bias):
    channels, width_all = source.shape
    images = width_all // (SIDE * SIDE)
    blocks = source.reshape(channels // GROUP_CH, GROUP_CH, images, SIDE * SIDE)
    mean_val = lax.optimization_barrier(jnp.mean(blocks, axis=(1, 3), keepdims=True))
    centred = blocks - mean_val
    var_val = lax.optimization_barrier(jnp.mean(centred * centred, axis=(1, 3), keepdims=True))
    inv_dev = lax.rsqrt(var_val + EPS_NORM)
    normed = (centred * inv_dev).reshape(channels, width_all)
    pre_act = normed * norm_gain[:, None] + norm_bias[:, None]
    return (normed, inv_dev, pre_act)

def group_backward(grad_act, pre_act, normed, inv_dev, norm_gain):
    channels, width_all = grad_act.shape
    images = width_all // (SIDE * SIDE)
    shape_four = (channels // GROUP_CH, GROUP_CH, images, SIDE * SIDE)
    sigmoid_val = jax.nn.sigmoid(pre_act)
    grad_pre = grad_act * sigmoid_val * (1.0 + pre_act * (1.0 - sigmoid_val))
    grad_norm = (grad_pre * norm_gain[:, None]).reshape(shape_four)
    normed_four = normed.reshape(shape_four)
    mean_first = lax.optimization_barrier(jnp.mean(grad_norm, axis=(1, 3), keepdims=True))
    mean_second = lax.optimization_barrier(jnp.mean(grad_norm * normed_four, axis=(1, 3), keepdims=True))
    return (inv_dev * (grad_norm - mean_first - normed_four * mean_second)).reshape(channels, width_all)

def adam_update(conv_weight, moment_one, moment_two, gradient):
    first_new = BETA_ONE * moment_one + (1.0 - BETA_ONE) * gradient
    second_new = BETA_TWO * moment_two + (1.0 - BETA_TWO) * gradient * gradient
    weight_new = conv_weight - LEARN_RATE * (first_new / CORRECT_ONE) / (jnp.sqrt(second_new / CORRECT_TWO) + EPS_ADAM)
    return (weight_new, first_new, second_new)

def reference(inputs, norm_gain, norm_bias, conv_weight, moment_one, moment_two, out_grad):
    weight_half = conv_weight.astype(jnp.bfloat16)
    group_width = IMG_GRP * SIDE * SIDE
    grouped_in = inputs.reshape(CHANNELS, N_DP, group_width).transpose(1, 0, 2)
    grouped_grad = out_grad.reshape(CHANNELS, N_DP, group_width).transpose(1, 0, 2)

    def per_group(grad_total, pair):
        source, upstream = pair
        normed, inv_dev, pre_act = group_stats(source, norm_gain, norm_bias)
        activation = jax.nn.silu(pre_act).astype(jnp.bfloat16)
        grad_half = upstream.astype(jnp.bfloat16)
        conv_out = jnp.zeros(source.shape, jnp.float32)
        grad_act = jnp.zeros(source.shape, jnp.float32)
        grad_taps = []
        for tap_index, (row_step, col_step) in enumerate(OFFSETS):
            moved = shifted(activation, row_step, col_step)
            conv_out = conv_out + jnp.dot(weight_half[tap_index], moved, preferred_element_type=jnp.float32)
            grad_taps.append(lax.dot_general(grad_half, moved, (((1,), (1,)), ((), ())), preferred_element_type=jnp.float32))
            back_term = lax.dot_general(weight_half[tap_index], grad_half, (((0,), (0,)), ((), ())), preferred_element_type=jnp.float32)
            grad_act = grad_act + shifted(back_term, -row_step, -col_step)
        block_out = source + conv_out
        input_grad = upstream + group_backward(grad_act, pre_act, normed, inv_dev, norm_gain)
        return (grad_total + jnp.stack(grad_taps), (block_out, input_grad))
    start_total = jnp.zeros((9, CHANNELS, CHANNELS), jnp.float32)
    grad_total, (outs_grouped, grads_grouped) = lax.scan(per_group, start_total, (grouped_in, grouped_grad))
    block_out = outs_grouped.transpose(1, 0, 2).reshape(CHANNELS, PIXELS)
    input_grad = grads_grouped.transpose(1, 0, 2).reshape(CHANNELS, PIXELS)
    gradient = grad_total / (IMG_GRP * N_DP)
    new_weight, new_moment_one, new_moment_two = adam_update(conv_weight, moment_one, moment_two, gradient)
    return (block_out, input_grad, new_weight, new_moment_one, new_moment_two)
```

```python
import jax
import jax.numpy as jnp
from jax import lax
from jax.experimental import pallas as pl
from jax.experimental.pallas import tpu as pltpu
from jax.sharding import Mesh, PartitionSpec as P

GROUP_CH = 40
SIDE = 32
ROWS_PAD = 32

EPS_NORM = 1e-05
BETA_ONE = 0.9
BETA_TWO = 0.999
CORRECT_ONE = 1.0 - 0.9**10
CORRECT_TWO = 1.0 - 0.999**10
LEARN_RATE = 0.001
EPS_ADAM = 1e-08
OFFSETS = ((-1, -1), (-1, 0), (-1, 1), (0, -1), (0, 0), (0, 1), (1, -1), (1, 0), (1, 1))

DP = ("z", "yl")
FSDP = ("x", "yh", "c")


def shifted(source, a, b):
    if a == 0 and b == 0:
        return source
    width = source.shape[-1]
    position = lax.broadcasted_iota(jnp.int32, (1, width), 1)
    row, col = position // SIDE, position % SIDE
    inside = (row + a >= 0) & (row + a < SIDE) & (col + b >= 0) & (col + b < SIDE)
    moved = pltpu.roll(source, (-(a * SIDE + b)) % width, 1)
    return jnp.where(inside, moved, 0.0)


def column(row):
    n = row.shape[1]
    eye = lax.broadcasted_iota(jnp.int32, (n, n), 0) == lax.broadcasted_iota(jnp.int32, (n, n), 1)
    return jnp.sum(jnp.where(eye, row, 0.0), axis=1, keepdims=True)


def norm_kernel(x_ref, gain_ref, bias_ref, act_ref, normed_ref, pre_ref, inv_ref):
    x = x_ref[...]
    count = x.shape[0] * x.shape[1]
    mean = jnp.sum(jnp.sum(x, axis=0, keepdims=True), axis=1, keepdims=True) / count
    centred = x - mean
    var = jnp.sum(jnp.sum(centred * centred, axis=0, keepdims=True), axis=1, keepdims=True) / count
    inv = lax.rsqrt(var + EPS_NORM)
    normed = centred * inv
    pre = normed * column(gain_ref[...]) + column(bias_ref[...])
    normed_ref[...] = normed
    pre_ref[...] = pre
    inv_ref[...] = jnp.broadcast_to(inv, inv_ref.shape)
    act_ref[...] = (pre * jax.nn.sigmoid(pre)).astype(jnp.bfloat16)


def nine_kernel(g_ref, out_ref):
    g = g_ref[...].astype(jnp.bfloat16).astype(jnp.float32)
    rows = g.shape[0]
    for tap, (a, b) in enumerate(OFFSETS):
        out_ref[tap * rows : (tap + 1) * rows, :] = shifted(g, -a, -b).astype(jnp.bfloat16)
    rest = out_ref.shape[0] - 9 * rows
    out_ref[9 * rows :, :] = jnp.zeros((rest, g.shape[1]), jnp.bfloat16)


def forward_kernel(w_ref, act_ref, x_ref, out_ref):
    rows = x_ref.shape[0]
    products = jnp.dot(w_ref[...], act_ref[...], preferred_element_type=jnp.float32)
    total = x_ref[...]
    for tap, (a, b) in enumerate(OFFSETS):
        total = total + shifted(products[tap * rows : (tap + 1) * rows, :], a, b)
    out_ref[...] = total


def back_kernel(parts_ref, normed_ref, pre_ref, inv_ref, gain_ref, grad_ref, out_ref):
    grad_act = jnp.sum(parts_ref[...].astype(jnp.float32), axis=0)
    pre, normed = pre_ref[...], normed_ref[...]
    s = jax.nn.sigmoid(pre)
    gn = grad_act * s * (1.0 + pre * (1.0 - s)) * column(gain_ref[...])
    count = gn.shape[0] * gn.shape[1]
    first = jnp.sum(jnp.sum(gn, axis=0, keepdims=True), axis=1, keepdims=True) / count
    second = jnp.sum(jnp.sum(gn * normed, axis=0, keepdims=True), axis=1, keepdims=True) / count
    out_ref[...] = grad_ref[...] + inv_ref[0:1, 0:1] * (gn - first - normed * second)


def body(inputs, norm_gain, norm_bias, conv_weight, moment_one, moment_two, out_grad):
    local_ch, width = inputs.shape
    n_fsdp = lax.axis_size(FSDP)
    n_z, n_yl, n_x = lax.axis_size("z"), lax.axis_size("yl"), lax.axis_size("x")
    n_dp = n_z * n_yl
    all_ch = local_ch * n_fsdp
    f32, bf16 = jnp.float32, jnp.bfloat16
    chunk_rows = -(-(9 * local_ch) // (8 * n_z)) * 8
    pad_rows = chunk_rows * n_z
    swap = [(0, 1), (1, 0)]
    gain_row, bias_row = norm_gain[None, :], norm_bias[None, :]

    tile = jax.ShapeDtypeStruct((local_ch, width), f32)
    act, normed, pre_act, inv = pl.pallas_call(
        norm_kernel,
        out_shape=(
            jax.ShapeDtypeStruct((local_ch, width), bf16), tile, tile,
            jax.ShapeDtypeStruct((8, 128), f32),
        ),
        name="norm",
    )(inputs, gain_row, bias_row)

    grad_rows = pl.pallas_call(
        nine_kernel, out_shape=jax.ShapeDtypeStruct((pad_rows, width), bf16), name="nine"
    )(out_grad)
    weight_nine = conv_weight.astype(bf16).reshape(9 * local_ch, all_ch)

    with jax.named_scope("act_yh"):
        other = lax.ppermute(act, "yh", swap)
    other, grad_rows, weight_nine = lax.optimization_barrier((other, grad_rows, weight_nine))
    mine = jnp.arange(2) == lax.axis_index("yh")
    pair = jnp.where(mine[:, None, None], act[None], other[None])
    with jax.named_scope("act_x"):
        by_x = lax.all_to_all(
            jnp.broadcast_to(pair[None], (n_x,) + pair.shape), "x", 0, 0, tiled=True
        )
    partial = lax.dot_general(
        weight_nine, grad_rows[: 9 * local_ch], (((0,), (0,)), ((), ())),
        preferred_element_type=f32,
    )
    partial = partial.astype(bf16).reshape(n_fsdp, local_ch, width)
    by_x, partial = lax.optimization_barrier((by_x, partial))
    by_x = by_x.reshape(n_x * 2, local_ch, width)
    with jax.named_scope("act_c"):
        other = lax.ppermute(by_x, "c", swap)
    mine = jnp.arange(2) == lax.axis_index("c")
    gathered = jnp.where(mine[None, :, None, None], by_x[:, None], other[:, None])
    gathered = gathered.reshape(all_ch, width)

    taps = lax.dot_general(
        grad_rows, gathered, (((1,), (1,)), ((), ())), preferred_element_type=f32
    )
    taps = taps.astype(bf16).reshape(n_z, chunk_rows, all_ch)
    with jax.named_scope("grad_z"):
        by_z = lax.all_to_all(taps, "z", 0, 0, tiled=True)

    block_out = pl.pallas_call(forward_kernel, out_shape=tile, name="forward")(
        weight_nine, gathered, inputs
    )
    by_z, block_out, partial = lax.optimization_barrier((by_z, block_out, partial))
    with jax.named_scope("back_f"):
        parts = lax.all_to_all(partial, FSDP, 0, 0, tiled=True)

    z_sum = jnp.sum(by_z.astype(f32), axis=0)
    with jax.named_scope("gather_yl"):
        by_yl = lax.all_gather(z_sum, "yl", axis=0)
    total = (jnp.sum(by_yl, axis=0) / n_dp).astype(bf16)
    with jax.named_scope("gather_z"):
        total = lax.all_gather(total, "z", axis=0, tiled=True)
    gradient = total[: 9 * local_ch].reshape(9, local_ch, all_ch).astype(f32)

    first_new = BETA_ONE * moment_one + (1.0 - BETA_ONE) * gradient
    second_new = BETA_TWO * moment_two + (1.0 - BETA_TWO) * gradient * gradient
    weight_new = conv_weight - LEARN_RATE * (first_new / CORRECT_ONE) / (
        jnp.sqrt(second_new / CORRECT_TWO) + EPS_ADAM
    )
    normed, weight_new = lax.optimization_barrier((normed, weight_new))
    input_grad = pl.pallas_call(back_kernel, out_shape=tile, name="back")(
        parts, normed, pre_act, inv, gain_row, out_grad
    )
    return (block_out, input_grad, weight_new, first_new, second_new)


def solution(mesh):
    five = Mesh(mesh.devices.reshape(12, 4, 4, 2, 2), ("z", "yl", "x", "yh", "c"))
    act, chan, wgt = P(FSDP, DP), P(FSDP), P(None, FSDP, None)
    return jax.shard_map(
        body,
        mesh=five,
        in_specs=(act, chan, chan, wgt, wgt, wgt, act),
        out_specs=(act, act, wgt, wgt, wgt),
        check_vma=False,
    )
```

```python
import jax
import jax.numpy as jnp
from jax import lax
from jax.experimental import pallas as pl
from jax.experimental.pallas import tpu as pltpu
from jax.sharding import Mesh, PartitionSpec as P

SIDE = 32

EPS_NORM = 1e-05
BETA_ONE = 0.9
BETA_TWO = 0.999
CORRECT_ONE = 1.0 - 0.9**10
CORRECT_TWO = 1.0 - 0.999**10
LEARN_RATE = 0.001
EPS_ADAM = 1e-08
OFFSETS = ((-1, -1), (-1, 0), (-1, 1), (0, -1), (0, 0), (0, 1), (1, -1), (1, 0), (1, 1))

DP = ("z", "yl")
FSDP = ("x", "yh", "c")
XY = ("x", "yh")


def shifted(source, a, b):
    if a == 0 and b == 0:
        return source
    width = source.shape[-1]
    position = lax.broadcasted_iota(jnp.int32, (1, width), 1)
    row, col = position // SIDE, position % SIDE
    inside = (row + a >= 0) & (row + a < SIDE) & (col + b >= 0) & (col + b < SIDE)
    moved = pltpu.roll(source, (-(a * SIDE + b)) % width, 1)
    return jnp.where(inside, moved, 0.0)


def column(row):
    n = row.shape[1]
    eye = lax.broadcasted_iota(jnp.int32, (n, n), 0) == lax.broadcasted_iota(jnp.int32, (n, n), 1)
    return jnp.sum(jnp.where(eye, row, 0.0), axis=1, keepdims=True)


def norm_kernel(x_ref, gain_ref, bias_ref, act_ref, normed_ref, pre_ref, inv_ref):
    x = x_ref[...]
    count = x.shape[0] * x.shape[1]
    mean = jnp.sum(jnp.sum(x, axis=0, keepdims=True), axis=1, keepdims=True) / count
    centred = x - mean
    var = jnp.sum(jnp.sum(centred * centred, axis=0, keepdims=True), axis=1, keepdims=True) / count
    inv = lax.rsqrt(var + EPS_NORM)
    normed = centred * inv
    pre = normed * column(gain_ref[...]) + column(bias_ref[...])
    normed_ref[...] = normed
    pre_ref[...] = pre
    inv_ref[...] = jnp.broadcast_to(inv, inv_ref.shape)
    act = (pre * jax.nn.sigmoid(pre)).astype(jnp.bfloat16)
    for copy in range(act_ref.shape[0]):
        act_ref[copy] = act


def nine_kernel(g_ref, out_ref):
    g = g_ref[...].astype(jnp.bfloat16).astype(jnp.float32)
    rows = g.shape[0]
    for tap, (a, b) in enumerate(OFFSETS):
        out_ref[tap * rows : (tap + 1) * rows, :] = shifted(g, -a, -b).astype(jnp.bfloat16)
    rest = out_ref.shape[0] - 9 * rows
    out_ref[9 * rows :, :] = jnp.zeros((rest, g.shape[1]), jnp.bfloat16)


def forward_kernel(w_ref, act_ref, x_ref, out_ref):
    rows = x_ref.shape[0]
    products = jnp.dot(w_ref[...], act_ref[...], preferred_element_type=jnp.float32)
    total = x_ref[...]
    for tap, (a, b) in enumerate(OFFSETS):
        total = total + shifted(products[tap * rows : (tap + 1) * rows, :], a, b)
    out_ref[...] = total


def back_kernel(parts_ref, normed_ref, pre_ref, inv_ref, gain_ref, grad_ref, out_ref):
    grad_act = jnp.sum(parts_ref[...].astype(jnp.float32), axis=0)
    pre, normed = pre_ref[...], normed_ref[...]
    s = jax.nn.sigmoid(pre)
    gn = grad_act * s * (1.0 + pre * (1.0 - s)) * column(gain_ref[...])
    count = gn.shape[0] * gn.shape[1]
    first = jnp.sum(jnp.sum(gn, axis=0, keepdims=True), axis=1, keepdims=True) / count
    second = jnp.sum(jnp.sum(gn * normed, axis=0, keepdims=True), axis=1, keepdims=True) / count
    out_ref[...] = grad_ref[...] + inv_ref[0:1, 0:1] * (gn - first - normed * second)


def step(inputs, norm_gain, norm_bias, conv_weight, moment_one, moment_two, out_grad):
    local_ch, width = inputs.shape
    n_fsdp = lax.axis_size(FSDP)
    n_z, n_yl = lax.axis_size("z"), lax.axis_size("yl")
    n_dp, n_xy = n_z * n_yl, lax.axis_size(XY)
    all_ch = local_ch * n_fsdp
    f32, bf16 = jnp.float32, jnp.bfloat16
    chunk_rows = -(-(9 * local_ch) // (8 * n_z)) * 8
    pad_rows = chunk_rows * n_z
    swap = [(0, 1), (1, 0)]
    gain_row, bias_row = norm_gain[None, :], norm_bias[None, :]

    tile = jax.ShapeDtypeStruct((local_ch, width), f32)
    act, normed, pre_act, inv = pl.pallas_call(
        norm_kernel,
        out_shape=(
            jax.ShapeDtypeStruct((n_xy, local_ch, width), bf16), tile, tile,
            jax.ShapeDtypeStruct((8, 128), f32),
        ),
        name="norm",
    )(inputs, gain_row, bias_row)

    grad_rows = pl.pallas_call(
        nine_kernel, out_shape=jax.ShapeDtypeStruct((pad_rows, width), bf16), name="nine"
    )(out_grad)
    weight_nine = conv_weight.astype(bf16).reshape(9 * local_ch, all_ch)

    by_xy = lax.all_to_all(act, XY, 0, 0, tiled=True)
    partial = lax.dot_general(
        weight_nine, grad_rows[: 9 * local_ch], (((0,), (0,)), ((), ())),
        preferred_element_type=f32,
    ).reshape(n_xy, 2, local_ch, width)
    core = lax.axis_index("c")
    keep = lax.dynamic_index_in_dim(partial, core, 1, keepdims=False)
    give = lax.dynamic_index_in_dim(partial, 1 - core, 1, keepdims=False)
    taken = lax.ppermute(give, "c", swap)
    partial = (keep + taken).astype(bf16)
    by_xy, partial = lax.optimization_barrier((by_xy, partial))
    other = lax.ppermute(by_xy, "c", swap)
    mine = jnp.arange(2) == core
    gathered = jnp.where(mine[None, :, None, None], by_xy[:, None], other[:, None])
    gathered = gathered.reshape(all_ch, width)

    taps = lax.dot_general(
        grad_rows, gathered, (((1,), (1,)), ((), ())), preferred_element_type=f32
    )
    taps = taps.astype(bf16).reshape(n_z, chunk_rows, all_ch)
    by_z = lax.all_to_all(taps, "z", 0, 0, tiled=True)

    block_out = pl.pallas_call(forward_kernel, out_shape=tile, name="forward")(
        weight_nine, gathered, inputs
    )
    by_z, block_out = lax.optimization_barrier((by_z, block_out))
    z_sum = jnp.sum(by_z.astype(f32), axis=0)
    by_yl = lax.all_gather(z_sum, "yl", axis=0)
    by_yl, partial = lax.optimization_barrier((by_yl, partial))
    parts = lax.all_to_all(partial, XY, 0, 0, tiled=True)
    total = (jnp.sum(by_yl, axis=0) / n_dp).astype(bf16)
    total = lax.all_gather(total, "z", axis=0, tiled=True)
    gradient = total[: 9 * local_ch].reshape(9, local_ch, all_ch).astype(f32)

    first_new = BETA_ONE * moment_one + (1.0 - BETA_ONE) * gradient
    second_new = BETA_TWO * moment_two + (1.0 - BETA_TWO) * gradient * gradient
    weight_new = conv_weight - LEARN_RATE * (first_new / CORRECT_ONE) / (
        jnp.sqrt(second_new / CORRECT_TWO) + EPS_ADAM
    )
    normed, weight_new = lax.optimization_barrier((normed, weight_new))
    input_grad = pl.pallas_call(back_kernel, out_shape=tile, name="back")(
        parts, normed, pre_act, inv, gain_row, out_grad
    )
    return (block_out, input_grad, weight_new, first_new, second_new)


def solution(mesh):
    five = Mesh(mesh.devices.reshape(12, 4, 4, 2, 2), ("z", "yl", "x", "yh", "c"))
    act, chan, wgt = P(FSDP, DP), P(FSDP), P(None, FSDP, None)
    return jax.shard_map(
        step,
        mesh=five,
        in_specs=(act, chan, chan, wgt, wgt, wgt, act),
        out_specs=(act, act, wgt, wgt, wgt),
        check_vma=False,
    )
```

```python
import jax
import jax.numpy as jnp
from jax import lax
from jax.experimental import pallas as pl
from jax.experimental.pallas import tpu as pltpu
from jax.sharding import Mesh, PartitionSpec as P

SIDE = 32

EPS_NORM = 1e-05
BETA_ONE = 0.9
BETA_TWO = 0.999
CORRECT_ONE = 1.0 - 0.9**10
CORRECT_TWO = 1.0 - 0.999**10
LEARN_RATE = 0.001
EPS_ADAM = 1e-08
OFFSETS = ((-1, -1), (-1, 0), (-1, 1), (0, -1), (0, 0), (0, 1), (1, -1), (1, 0), (1, 1))

DP = ("z", "yl")
FSDP = ("x", "yh", "c")
XY = ("x", "yh")


def shifted(source, a, b):
    if a == 0 and b == 0:
        return source
    width = source.shape[-1]
    position = lax.broadcasted_iota(jnp.int32, (1, width), 1)
    row, col = position // SIDE, position % SIDE
    inside = (row + a >= 0) & (row + a < SIDE) & (col + b >= 0) & (col + b < SIDE)
    moved = pltpu.roll(source, (-(a * SIDE + b)) % width, 1)
    return jnp.where(inside, moved, 0.0)


def column(row):
    n = row.shape[1]
    eye = lax.broadcasted_iota(jnp.int32, (n, n), 0) == lax.broadcasted_iota(jnp.int32, (n, n), 1)
    return jnp.sum(jnp.where(eye, row, 0.0), axis=1, keepdims=True)


def norm_kernel(x_ref, gain_ref, bias_ref, act_ref, normed_ref, pre_ref, inv_ref):
    x = x_ref[...]
    count = x.shape[0] * x.shape[1]
    mean = jnp.sum(jnp.sum(x, axis=0, keepdims=True), axis=1, keepdims=True) / count
    centred = x - mean
    var = jnp.sum(jnp.sum(centred * centred, axis=0, keepdims=True), axis=1, keepdims=True) / count
    inv = lax.rsqrt(var + EPS_NORM)
    normed = centred * inv
    pre = normed * column(gain_ref[...]) + column(bias_ref[...])
    normed_ref[...] = normed
    pre_ref[...] = pre
    inv_ref[...] = jnp.broadcast_to(inv, inv_ref.shape)
    act = (pre * jax.nn.sigmoid(pre)).astype(jnp.bfloat16)
    for copy in range(act_ref.shape[0]):
        act_ref[copy] = act


def nine_kernel(g_ref, out_ref):
    g = g_ref[...].astype(jnp.bfloat16).astype(jnp.float32)
    rows = g.shape[0]
    for tap, (a, b) in enumerate(OFFSETS):
        out_ref[tap * rows : (tap + 1) * rows, :] = shifted(g, -a, -b).astype(jnp.bfloat16)
    rest = out_ref.shape[0] - 9 * rows
    out_ref[9 * rows :, :] = jnp.zeros((rest, g.shape[1]), jnp.bfloat16)


def forward_kernel(w_ref, act_ref, x_ref, out_ref):
    rows = x_ref.shape[0]
    products = jnp.dot(w_ref[...], act_ref[...], preferred_element_type=jnp.float32)
    total = x_ref[...]
    for tap, (a, b) in enumerate(OFFSETS):
        total = total + shifted(products[tap * rows : (tap + 1) * rows, :], a, b)
    out_ref[...] = total


def back_kernel(keep_ref, taken_ref, normed_ref, pre_ref, inv_ref, gain_ref, grad_ref, out_ref):
    grad_act = keep_ref[...].astype(jnp.float32) + taken_ref[...].astype(jnp.float32)
    pre, normed = pre_ref[...], normed_ref[...]
    s = jax.nn.sigmoid(pre)
    gn = grad_act * s * (1.0 + pre * (1.0 - s)) * column(gain_ref[...])
    count = gn.shape[0] * gn.shape[1]
    first = jnp.sum(jnp.sum(gn, axis=0, keepdims=True), axis=1, keepdims=True) / count
    second = jnp.sum(jnp.sum(gn * normed, axis=0, keepdims=True), axis=1, keepdims=True) / count
    out_ref[...] = grad_ref[...] + inv_ref[0:1, 0:1] * (gn - first - normed * second)


def step(inputs, norm_gain, norm_bias, conv_weight, moment_one, moment_two, out_grad):
    local_ch, width = inputs.shape
    n_fsdp = lax.axis_size(FSDP)
    n_z, n_yl, n_x = lax.axis_size("z"), lax.axis_size("yl"), lax.axis_size("x")
    n_dp, n_xy = n_z * n_yl, lax.axis_size(XY)
    all_ch = local_ch * n_fsdp
    f32, bf16 = jnp.float32, jnp.bfloat16
    chunk_rows = -(-(9 * local_ch) // (8 * n_z)) * 8
    pad_rows = chunk_rows * n_z
    swap = [(0, 1), (1, 0)]
    gain_row, bias_row = norm_gain[None, :], norm_bias[None, :]

    tile = jax.ShapeDtypeStruct((local_ch, width), f32)
    act, normed, pre_act, inv = pl.pallas_call(
        norm_kernel,
        out_shape=(
            jax.ShapeDtypeStruct((n_xy, local_ch, width), bf16), tile, tile,
            jax.ShapeDtypeStruct((8, 128), f32),
        ),
        name="norm",
    )(inputs, gain_row, bias_row)

    grad_rows = pl.pallas_call(
        nine_kernel, out_shape=jax.ShapeDtypeStruct((pad_rows, width), bf16), name="nine"
    )(out_grad)
    weight_nine = conv_weight.astype(bf16).reshape(9 * local_ch, all_ch)

    by_xy = lax.all_to_all(act, XY, 0, 0, tiled=True)
    partial = lax.dot_general(
        weight_nine, grad_rows[: 9 * local_ch], (((0,), (0,)), ((), ())),
        preferred_element_type=f32,
    ).reshape(n_xy, 2, local_ch, width)
    core = lax.axis_index("c")
    keep = lax.dynamic_index_in_dim(partial, core, 1, keepdims=False)
    give = lax.dynamic_index_in_dim(partial, 1 - core, 1, keepdims=False)
    taken = lax.ppermute(give, "c", swap)
    partial = (keep + taken).astype(bf16)
    by_xy, partial = lax.optimization_barrier((by_xy, partial))
    other = lax.ppermute(by_xy, "c", swap)
    mine = jnp.arange(2) == core
    gathered = jnp.where(mine[None, :, None, None], by_xy[:, None], other[:, None])
    gathered = gathered.reshape(all_ch, width)

    taps = lax.dot_general(
        grad_rows, gathered, (((1,), (1,)), ((), ())), preferred_element_type=f32
    )
    taps = taps.astype(bf16).reshape(n_z, chunk_rows, all_ch)
    by_z = lax.all_to_all(taps, "z", 0, 0, tiled=True)

    block_out = pl.pallas_call(forward_kernel, out_shape=tile, name="forward")(
        weight_nine, gathered, inputs
    )
    at = lax.axis_index("x")
    by_chip = partial.reshape(n_x, 2, local_ch, width)
    pick = lambda k: lax.dynamic_index_in_dim(by_chip, lax.rem(at + k, n_x), 0, keepdims=False)
    moved = [
        lax.ppermute(pick(k), "x", [(i, (i + k) % n_x) for i in range(n_x)])
        for k in range(1, n_x)
    ]
    pair = sum((m.astype(f32) for m in moved), pick(0).astype(f32)).astype(bf16)
    row = lax.axis_index("yh")
    taken = lax.ppermute(
        lax.dynamic_index_in_dim(pair, 1 - row, 0, keepdims=False), "yh", swap
    )
    keep = lax.dynamic_index_in_dim(pair, row, 0, keepdims=False)
    input_grad = pl.pallas_call(back_kernel, out_shape=tile, name="back")(
        keep, taken, normed, pre_act, inv, gain_row, out_grad
    )

    z_sum = jnp.sum(by_z.astype(f32), axis=0)
    by_yl = lax.all_to_all(
        jnp.broadcast_to(z_sum[None], (n_yl,) + z_sum.shape), "yl", 0, 0, tiled=True
    )
    total = (jnp.sum(by_yl, axis=0) / n_dp).astype(bf16)
    total = lax.all_gather(total, "z", axis=0, tiled=True)
    gradient = total[: 9 * local_ch].reshape(9, local_ch, all_ch).astype(f32)

    first_new = BETA_ONE * moment_one + (1.0 - BETA_ONE) * gradient
    second_new = BETA_TWO * moment_two + (1.0 - BETA_TWO) * gradient * gradient
    weight_new = conv_weight - LEARN_RATE * (first_new / CORRECT_ONE) / (
        jnp.sqrt(second_new / CORRECT_TWO) + EPS_ADAM
    )
    return (block_out, input_grad, weight_new, first_new, second_new)


def solution(mesh):
    five = Mesh(mesh.devices.reshape(12, 4, 4, 2, 2), ("z", "yl", "x", "yh", "c"))
    act, chan, wgt = P(FSDP, DP), P(FSDP), P(None, FSDP, None)
    return jax.shard_map(
        step,
        mesh=five,
        in_specs=(act, chan, chan, wgt, wgt, wgt, act),
        out_specs=(act, act, wgt, wgt, wgt),
        check_vma=False,
    )
```

```python
import jax
import jax.numpy as jnp
from jax import lax
from jax.experimental import pallas as pl
from jax.experimental.pallas import tpu as pltpu
from jax.sharding import Mesh, PartitionSpec as P

SIDE = 32

EPS_NORM = 1e-05
BETA_ONE = 0.9
BETA_TWO = 0.999
CORRECT_ONE = 1.0 - 0.9**10
CORRECT_TWO = 1.0 - 0.999**10
LEARN_RATE = 0.001
EPS_ADAM = 1e-08
OFFSETS = ((-1, -1), (-1, 0), (-1, 1), (0, -1), (0, 0), (0, 1), (1, -1), (1, 0), (1, 1))

DP = ("z", "yl")
FSDP = ("x", "yh", "c")
XY = ("x", "yh")


def shifted(source, a, b):
    if a == 0 and b == 0:
        return source
    width = source.shape[-1]
    position = lax.broadcasted_iota(jnp.int32, (1, width), 1)
    row, col = position // SIDE, position % SIDE
    inside = (row + a >= 0) & (row + a < SIDE) & (col + b >= 0) & (col + b < SIDE)
    moved = pltpu.roll(source, (-(a * SIDE + b)) % width, 1)
    return jnp.where(inside, moved, 0.0)


def column(row):
    n = row.shape[1]
    eye = lax.broadcasted_iota(jnp.int32, (n, n), 0) == lax.broadcasted_iota(jnp.int32, (n, n), 1)
    return jnp.sum(jnp.where(eye, row, 0.0), axis=1, keepdims=True)


def norm_kernel(x_ref, gain_ref, bias_ref, act_ref, normed_ref, pre_ref, inv_ref):
    x = x_ref[...]
    count = x.shape[0] * x.shape[1]
    mean = jnp.sum(jnp.sum(x, axis=0, keepdims=True), axis=1, keepdims=True) / count
    centred = x - mean
    var = jnp.sum(jnp.sum(centred * centred, axis=0, keepdims=True), axis=1, keepdims=True) / count
    inv = lax.rsqrt(var + EPS_NORM)
    normed = centred * inv
    pre = normed * column(gain_ref[...]) + column(bias_ref[...])
    normed_ref[...] = normed
    pre_ref[...] = pre
    inv_ref[...] = jnp.broadcast_to(inv, inv_ref.shape)
    act = (pre * jax.nn.sigmoid(pre)).astype(jnp.bfloat16)
    for copy in range(act_ref.shape[0]):
        act_ref[copy] = act


def nine_kernel(g_ref, out_ref):
    g = g_ref[...].astype(jnp.bfloat16).astype(jnp.float32)
    rows = g.shape[0]
    for tap, (a, b) in enumerate(OFFSETS):
        out_ref[tap * rows : (tap + 1) * rows, :] = shifted(g, -a, -b).astype(jnp.bfloat16)
    rest = out_ref.shape[0] - 9 * rows
    out_ref[9 * rows :, :] = jnp.zeros((rest, g.shape[1]), jnp.bfloat16)


def forward_kernel(w_ref, act_ref, x_ref, out_ref):
    rows = x_ref.shape[0]
    products = jnp.dot(w_ref[...], act_ref[...], preferred_element_type=jnp.float32)
    total = x_ref[...]
    for tap, (a, b) in enumerate(OFFSETS):
        total = total + shifted(products[tap * rows : (tap + 1) * rows, :], a, b)
    out_ref[...] = total


def back_kernel(keep_ref, taken_ref, normed_ref, pre_ref, inv_ref, gain_ref, grad_ref, out_ref):
    grad_act = keep_ref[...].astype(jnp.float32) + taken_ref[...].astype(jnp.float32)
    pre, normed = pre_ref[...], normed_ref[...]
    s = jax.nn.sigmoid(pre)
    gn = grad_act * s * (1.0 + pre * (1.0 - s)) * column(gain_ref[...])
    count = gn.shape[0] * gn.shape[1]
    first = jnp.sum(jnp.sum(gn, axis=0, keepdims=True), axis=1, keepdims=True) / count
    second = jnp.sum(jnp.sum(gn * normed, axis=0, keepdims=True), axis=1, keepdims=True) / count
    out_ref[...] = grad_ref[...] + inv_ref[0:1, 0:1] * (gn - first - normed * second)


def step(inputs, norm_gain, norm_bias, conv_weight, moment_one, moment_two, out_grad):
    local_ch, width = inputs.shape
    n_fsdp = lax.axis_size(FSDP)
    n_z, n_yl, n_x = lax.axis_size("z"), lax.axis_size("yl"), lax.axis_size("x")
    n_dp, n_xy = n_z * n_yl, lax.axis_size(XY)
    all_ch = local_ch * n_fsdp
    f32, bf16 = jnp.float32, jnp.bfloat16
    chunk_rows = -(-(9 * local_ch) // (8 * n_z)) * 8
    pad_rows = chunk_rows * n_z
    swap = [(0, 1), (1, 0)]
    gain_row, bias_row = norm_gain[None, :], norm_bias[None, :]

    tile = jax.ShapeDtypeStruct((local_ch, width), f32)
    act, normed, pre_act, inv = pl.pallas_call(
        norm_kernel,
        out_shape=(
            jax.ShapeDtypeStruct((n_xy, local_ch, width), bf16), tile, tile,
            jax.ShapeDtypeStruct((8, 128), f32),
        ),
        name="norm",
    )(inputs, gain_row, bias_row)

    grad_rows = pl.pallas_call(
        nine_kernel, out_shape=jax.ShapeDtypeStruct((pad_rows, width), bf16), name="nine"
    )(out_grad)
    weight_nine = conv_weight.astype(bf16).reshape(9 * local_ch, all_ch)

    by_xy = lax.all_to_all(act, XY, 0, 0, tiled=True)
    core = lax.axis_index("c")
    partial = lax.dot_general(
        weight_nine, grad_rows[: 9 * local_ch], (((0,), (0,)), ((), ())),
        preferred_element_type=f32,
    ).reshape(n_xy, 2, local_ch, width)
    give = lax.dynamic_index_in_dim(partial, 1 - core, 1, keepdims=False)
    by_xy, partial, give, weight_nine = lax.optimization_barrier(
        (by_xy, partial, give, weight_nine)
    )
    other = lax.ppermute(by_xy, "c", swap)
    mine = jnp.arange(2) == core
    gathered = jnp.where(mine[None, :, None, None], by_xy[:, None], other[:, None])
    gathered = gathered.reshape(all_ch, width)

    taps = lax.dot_general(
        grad_rows, gathered, (((1,), (1,)), ((), ())), preferred_element_type=f32
    )
    taps = taps.astype(bf16).reshape(n_z, chunk_rows, all_ch)
    by_z = lax.all_to_all(taps, "z", 0, 0, tiled=True)

    block_out = pl.pallas_call(forward_kernel, out_shape=tile, name="forward")(
        weight_nine, gathered, inputs
    )
    keep = lax.dynamic_index_in_dim(partial, core, 1, keepdims=False)
    taken = lax.ppermute(give, "c", swap)
    partial = (keep + taken).astype(bf16)
    at = lax.axis_index("x")
    by_chip = partial.reshape(n_x, 2, local_ch, width)
    pick = lambda k: lax.dynamic_index_in_dim(by_chip, lax.rem(at + k, n_x), 0, keepdims=False)
    moved = [
        lax.ppermute(pick(k), "x", [(i, (i + k) % n_x) for i in range(n_x)])
        for k in range(1, n_x)
    ]
    pair = sum((m.astype(f32) for m in moved), pick(0).astype(f32)).astype(bf16)
    row = lax.axis_index("yh")
    taken = lax.ppermute(
        lax.dynamic_index_in_dim(pair, 1 - row, 0, keepdims=False), "yh", swap
    )
    keep = lax.dynamic_index_in_dim(pair, row, 0, keepdims=False)
    input_grad = pl.pallas_call(back_kernel, out_shape=tile, name="back")(
        keep, taken, normed, pre_act, inv, gain_row, out_grad
    )

    z_sum = jnp.sum(by_z.astype(f32), axis=0)
    by_yl = lax.all_to_all(
        jnp.broadcast_to(z_sum[None], (n_yl,) + z_sum.shape), "yl", 0, 0, tiled=True
    )
    total = (jnp.sum(by_yl, axis=0) / n_dp).astype(bf16)
    total = lax.all_to_all(
        jnp.broadcast_to(total[None], (n_z,) + total.shape), "z", 0, 0, tiled=True
    )
    gradient = total.reshape(pad_rows, all_ch)[: 9 * local_ch].reshape(9, local_ch, all_ch).astype(f32)

    first_new = BETA_ONE * moment_one + (1.0 - BETA_ONE) * gradient
    second_new = BETA_TWO * moment_two + (1.0 - BETA_TWO) * gradient * gradient
    weight_new = conv_weight - LEARN_RATE * (first_new / CORRECT_ONE) / (
        jnp.sqrt(second_new / CORRECT_TWO) + EPS_ADAM
    )
    return (block_out, input_grad, weight_new, first_new, second_new)


def solution(mesh):
    five = Mesh(mesh.devices.reshape(12, 4, 4, 2, 2), ("z", "yl", "x", "yh", "c"))
    act, chan, wgt = P(FSDP, DP), P(FSDP), P(None, FSDP, None)
    return jax.shard_map(
        step,
        mesh=five,
        in_specs=(act, chan, chan, wgt, wgt, wgt, act),
        out_specs=(act, act, wgt, wgt, wgt),
        check_vma=False,
    )
```

```python
import functools

import jax
import jax.numpy as jnp
from jax import lax
from jax.experimental import pallas as pl
from jax.experimental.pallas import tpu as pltpu
from jax.sharding import Mesh, PartitionSpec as P

SIDE = 32

EPS_NORM = 1e-05
BETA_ONE = 0.9
BETA_TWO = 0.999
CORRECT_ONE = 1.0 - 0.9**10
CORRECT_TWO = 1.0 - 0.999**10
LEARN_RATE = 0.001
EPS_ADAM = 1e-08
OFFSETS = ((-1, -1), (-1, 0), (-1, 1), (0, -1), (0, 0), (0, 1), (1, -1), (1, 0), (1, 1))

SMALL = pltpu.CompilerParams(vmem_limit_bytes=16 * 2**20)
DP = ("z", "yl")
FSDP = ("x", "yh", "c")
XY = ("x", "yh")


def shifted(source, a, b):
    if a == 0 and b == 0:
        return source
    width = source.shape[-1]
    position = lax.broadcasted_iota(jnp.int32, (1, width), 1)
    row, col = position // SIDE, position % SIDE
    inside = (row + a >= 0) & (row + a < SIDE) & (col + b >= 0) & (col + b < SIDE)
    moved = pltpu.roll(source, (-(a * SIDE + b)) % width, 1)
    return jnp.where(inside, moved, 0.0)


def column(row):
    n = row.shape[1]
    eye = lax.broadcasted_iota(jnp.int32, (n, n), 0) == lax.broadcasted_iota(jnp.int32, (n, n), 1)
    return jnp.sum(jnp.where(eye, row, 0.0), axis=1, keepdims=True)


def norm_kernel(x_ref, gain_ref, bias_ref, act_ref, normed_ref, pre_ref, inv_ref):
    x = x_ref[...]
    count = x.shape[0] * x.shape[1]
    mean = jnp.sum(jnp.sum(x, axis=0, keepdims=True), axis=1, keepdims=True) / count
    centred = x - mean
    var = jnp.sum(jnp.sum(centred * centred, axis=0, keepdims=True), axis=1, keepdims=True) / count
    inv = lax.rsqrt(var + EPS_NORM)
    normed = centred * inv
    pre = normed * column(gain_ref[...]) + column(bias_ref[...])
    normed_ref[...] = normed
    pre_ref[...] = pre
    inv_ref[...] = jnp.broadcast_to(inv, inv_ref.shape)
    act = (pre * jax.nn.sigmoid(pre)).astype(jnp.bfloat16)
    for copy in range(act_ref.shape[0]):
        act_ref[copy] = act


def nine_kernel(g_ref, out_ref):
    g = g_ref[...].astype(jnp.bfloat16).astype(jnp.float32)
    rows = g.shape[0]
    for tap, (a, b) in enumerate(OFFSETS):
        out_ref[tap * rows : (tap + 1) * rows, :] = shifted(g, -a, -b).astype(jnp.bfloat16)
    rest = out_ref.shape[0] - 9 * rows
    out_ref[9 * rows :, :] = jnp.zeros((rest, g.shape[1]), jnp.bfloat16)


def forward_kernel(w_ref, act_ref, x_ref, out_ref):
    rows = x_ref.shape[0]
    products = jnp.dot(w_ref[...], act_ref[...], preferred_element_type=jnp.float32)
    total = x_ref[...]
    for tap, (a, b) in enumerate(OFFSETS):
        total = total + shifted(products[tap * rows : (tap + 1) * rows, :], a, b)
    out_ref[...] = total


def sum_copies_kernel(parts_ref, out_ref, *, scale):
    total = (jnp.sum(parts_ref[...].astype(jnp.float32), axis=0) * scale).astype(out_ref.dtype)
    for copy in range(out_ref.shape[0]):
        out_ref[copy] = total


def back_kernel(keep_ref, taken_ref, normed_ref, pre_ref, inv_ref, gain_ref, grad_ref, out_ref):
    grad_act = keep_ref[...].astype(jnp.float32) + taken_ref[...].astype(jnp.float32)
    pre, normed = pre_ref[...], normed_ref[...]
    s = jax.nn.sigmoid(pre)
    gn = grad_act * s * (1.0 + pre * (1.0 - s)) * column(gain_ref[...])
    count = gn.shape[0] * gn.shape[1]
    first = jnp.sum(jnp.sum(gn, axis=0, keepdims=True), axis=1, keepdims=True) / count
    second = jnp.sum(jnp.sum(gn * normed, axis=0, keepdims=True), axis=1, keepdims=True) / count
    out_ref[...] = grad_ref[...] + inv_ref[0:1, 0:1] * (gn - first - normed * second)


def step(inputs, norm_gain, norm_bias, conv_weight, moment_one, moment_two, out_grad):
    local_ch, width = inputs.shape
    n_fsdp = lax.axis_size(FSDP)
    n_z, n_yl, n_x = lax.axis_size("z"), lax.axis_size("yl"), lax.axis_size("x")
    n_dp, n_xy = n_z * n_yl, lax.axis_size(XY)
    all_ch = local_ch * n_fsdp
    f32, bf16 = jnp.float32, jnp.bfloat16
    chunk_rows = -(-(9 * local_ch) // (8 * n_z)) * 8
    pad_rows = chunk_rows * n_z
    swap = [(0, 1), (1, 0)]
    gain_row, bias_row = norm_gain[None, :], norm_bias[None, :]

    tile = jax.ShapeDtypeStruct((local_ch, width), f32)
    act, normed, pre_act, inv = pl.pallas_call(
        norm_kernel,
        out_shape=(
            jax.ShapeDtypeStruct((n_xy, local_ch, width), bf16), tile, tile,
            jax.ShapeDtypeStruct((8, 128), f32),
        ),
        name="norm",
    )(inputs, gain_row, bias_row)

    grad_rows = pl.pallas_call(
        nine_kernel, out_shape=jax.ShapeDtypeStruct((pad_rows, width), bf16), name="nine", compiler_params=SMALL
    )(out_grad)
    weight_nine = conv_weight.astype(bf16).reshape(9 * local_ch, all_ch)

    by_xy = lax.all_to_all(act, XY, 0, 0, tiled=True)
    core = lax.axis_index("c")
    partial = lax.dot_general(
        weight_nine, grad_rows[: 9 * local_ch], (((0,), (0,)), ((), ())),
        preferred_element_type=f32,
    ).reshape(n_xy, 2, local_ch, width)
    give = lax.dynamic_index_in_dim(partial, 1 - core, 1, keepdims=False)
    by_xy, partial, give, weight_nine = lax.optimization_barrier(
        (by_xy, partial, give, weight_nine)
    )
    other = lax.ppermute(by_xy, "c", swap)
    mine = jnp.arange(2) == core
    gathered = jnp.where(mine[None, :, None, None], by_xy[:, None], other[:, None])
    gathered = gathered.reshape(all_ch, width)

    taps = lax.dot_general(
        grad_rows, gathered, (((1,), (1,)), ((), ())), preferred_element_type=f32
    )
    taps = taps.astype(bf16).reshape(n_z, chunk_rows, all_ch)
    by_z = lax.all_to_all(taps, "z", 0, 0, tiled=True)

    block_out = pl.pallas_call(forward_kernel, out_shape=tile, name="forward", compiler_params=SMALL)(
        weight_nine, gathered, inputs
    )
    keep = lax.dynamic_index_in_dim(partial, core, 1, keepdims=False)
    taken = lax.ppermute(give, "c", swap)
    partial = (keep + taken).astype(bf16)
    at = lax.axis_index("x")
    by_chip = partial.reshape(n_x, 2, local_ch, width)
    pick = lambda k: lax.dynamic_index_in_dim(by_chip, lax.rem(at + k, n_x), 0, keepdims=False)
    moved = [
        lax.ppermute(pick(k), "x", [(i, (i + k) % n_x) for i in range(n_x)])
        for k in range(1, n_x)
    ]
    pair = sum((m.astype(f32) for m in moved), pick(0).astype(f32)).astype(bf16)
    row = lax.axis_index("yh")
    taken = lax.ppermute(
        lax.dynamic_index_in_dim(pair, 1 - row, 0, keepdims=False), "yh", swap
    )
    keep = lax.dynamic_index_in_dim(pair, row, 0, keepdims=False)
    input_grad = pl.pallas_call(back_kernel, out_shape=tile, name="back", compiler_params=SMALL)(
        keep, taken, normed, pre_act, inv, gain_row, out_grad
    )

    z_sum = pl.pallas_call(
        functools.partial(sum_copies_kernel, scale=1.0),
        out_shape=jax.ShapeDtypeStruct((n_yl, chunk_rows, all_ch), f32),
        name="sum_z", compiler_params=SMALL,
    )(by_z)
    by_yl = lax.all_to_all(z_sum, "yl", 0, 0, tiled=True)
    total = pl.pallas_call(
        functools.partial(sum_copies_kernel, scale=1.0 / n_dp),
        out_shape=jax.ShapeDtypeStruct((n_z, chunk_rows, all_ch), bf16),
        name="sum_yl", compiler_params=SMALL,
    )(by_yl)
    total = lax.all_to_all(total, "z", 0, 0, tiled=True)
    gradient = total.reshape(pad_rows, all_ch)[: 9 * local_ch].reshape(9, local_ch, all_ch).astype(f32)

    first_new = BETA_ONE * moment_one + (1.0 - BETA_ONE) * gradient
    second_new = BETA_TWO * moment_two + (1.0 - BETA_TWO) * gradient * gradient
    weight_new = conv_weight - LEARN_RATE * (first_new / CORRECT_ONE) / (
        jnp.sqrt(second_new / CORRECT_TWO) + EPS_ADAM
    )
    return (block_out, input_grad, weight_new, first_new, second_new)


def solution(mesh):
    five = Mesh(mesh.devices.reshape(12, 4, 4, 2, 2), ("z", "yl", "x", "yh", "c"))
    act, chan, wgt = P(FSDP, DP), P(FSDP), P(None, FSDP, None)
    return jax.shard_map(
        step,
        mesh=five,
        in_specs=(act, chan, chan, wgt, wgt, wgt, act),
        out_specs=(act, act, wgt, wgt, wgt),
        check_vma=False,
    )
```

```python
import jax
import jax.numpy as jnp
from jax import lax
from jax.experimental import pallas as pl
from jax.experimental.pallas import tpu as pltpu
from jax.sharding import Mesh, PartitionSpec as P

SIDE = 32

EPS_NORM = 1e-05
BETA_ONE = 0.9
BETA_TWO = 0.999
CORRECT_ONE = 1.0 - 0.9**10
CORRECT_TWO = 1.0 - 0.999**10
LEARN_RATE = 0.001
EPS_ADAM = 1e-08
OFFSETS = ((-1, -1), (-1, 0), (-1, 1), (0, -1), (0, 0), (0, 1), (1, -1), (1, 0), (1, 1))

SMALL = pltpu.CompilerParams(vmem_limit_bytes=16 * 2**20)
DP = ("z", "yl")
FSDP = ("x", "yh", "c")
XY = ("x", "yh")


def shifted(source, a, b):
    if a == 0 and b == 0:
        return source
    width = source.shape[-1]
    position = lax.broadcasted_iota(jnp.int32, (1, width), 1)
    row, col = position // SIDE, position % SIDE
    inside = (row + a >= 0) & (row + a < SIDE) & (col + b >= 0) & (col + b < SIDE)
    moved = pltpu.roll(source, (-(a * SIDE + b)) % width, 1)
    return jnp.where(inside, moved, 0.0)


def column(row):
    n = row.shape[1]
    eye = lax.broadcasted_iota(jnp.int32, (n, n), 0) == lax.broadcasted_iota(jnp.int32, (n, n), 1)
    return jnp.sum(jnp.where(eye, row, 0.0), axis=1, keepdims=True)


def norm_kernel(x_ref, gain_ref, bias_ref, act_ref, normed_ref, pre_ref, inv_ref):
    x = x_ref[...]
    count = x.shape[0] * x.shape[1]
    mean = jnp.sum(jnp.sum(x, axis=0, keepdims=True), axis=1, keepdims=True) / count
    centred = x - mean
    var = jnp.sum(jnp.sum(centred * centred, axis=0, keepdims=True), axis=1, keepdims=True) / count
    inv = lax.rsqrt(var + EPS_NORM)
    normed = centred * inv
    pre = normed * column(gain_ref[...]) + column(bias_ref[...])
    normed_ref[...] = normed
    pre_ref[...] = pre
    inv_ref[...] = jnp.broadcast_to(inv, inv_ref.shape)
    act = (pre * jax.nn.sigmoid(pre)).astype(jnp.bfloat16)
    for copy in range(act_ref.shape[0]):
        act_ref[copy] = act


def nine_kernel(g_ref, out_ref):
    g = g_ref[...].astype(jnp.bfloat16).astype(jnp.float32)
    rows = g.shape[0]
    for tap, (a, b) in enumerate(OFFSETS):
        out_ref[tap * rows : (tap + 1) * rows, :] = shifted(g, -a, -b).astype(jnp.bfloat16)
    rest = out_ref.shape[0] - 9 * rows
    out_ref[9 * rows :, :] = jnp.zeros((rest, g.shape[1]), jnp.bfloat16)


def forward_kernel(w_ref, act_ref, x_ref, out_ref):
    rows = x_ref.shape[0]
    products = jnp.dot(w_ref[...], act_ref[...], preferred_element_type=jnp.float32)
    total = x_ref[...]
    for tap, (a, b) in enumerate(OFFSETS):
        total = total + shifted(products[tap * rows : (tap + 1) * rows, :], a, b)
    out_ref[...] = total


def sum_copies_kernel(parts_ref, out_ref):
    total = jnp.sum(parts_ref[...].astype(jnp.float32), axis=0).astype(out_ref.dtype)
    for copy in range(out_ref.shape[0]):
        out_ref[copy] = total


def back_kernel(keep_ref, taken_ref, normed_ref, pre_ref, inv_ref, gain_ref, grad_ref, out_ref):
    grad_act = keep_ref[...].astype(jnp.float32) + taken_ref[...].astype(jnp.float32)
    pre, normed = pre_ref[...], normed_ref[...]
    s = jax.nn.sigmoid(pre)
    gn = grad_act * s * (1.0 + pre * (1.0 - s)) * column(gain_ref[...])
    count = gn.shape[0] * gn.shape[1]
    first = jnp.sum(jnp.sum(gn, axis=0, keepdims=True), axis=1, keepdims=True) / count
    second = jnp.sum(jnp.sum(gn * normed, axis=0, keepdims=True), axis=1, keepdims=True) / count
    out_ref[...] = grad_ref[...] + inv_ref[0:1, 0:1] * (gn - first - normed * second)


def step(inputs, norm_gain, norm_bias, conv_weight, moment_one, moment_two, out_grad):
    local_ch, width = inputs.shape
    n_fsdp = lax.axis_size(FSDP)
    n_z, n_yl, n_x = lax.axis_size("z"), lax.axis_size("yl"), lax.axis_size("x")
    n_dp, n_xy = n_z * n_yl, lax.axis_size(XY)
    all_ch = local_ch * n_fsdp
    f32, bf16 = jnp.float32, jnp.bfloat16
    chunk_rows = -(-(9 * local_ch) // (8 * n_z)) * 8
    pad_rows = chunk_rows * n_z
    swap = [(0, 1), (1, 0)]
    gain_row, bias_row = norm_gain[None, :], norm_bias[None, :]

    tile = jax.ShapeDtypeStruct((local_ch, width), f32)
    act, normed, pre_act, inv = pl.pallas_call(
        norm_kernel,
        out_shape=(
            jax.ShapeDtypeStruct((n_xy, local_ch, width), bf16), tile, tile,
            jax.ShapeDtypeStruct((8, 128), f32),
        ),
        name="norm",
    )(inputs, gain_row, bias_row)

    grad_rows = pl.pallas_call(
        nine_kernel, out_shape=jax.ShapeDtypeStruct((pad_rows, width), bf16), name="nine", compiler_params=SMALL
    )(out_grad)
    weight_nine = conv_weight.astype(bf16).reshape(9 * local_ch, all_ch)

    by_xy = lax.all_to_all(act, XY, 0, 0, tiled=True)
    core = lax.axis_index("c")
    partial = lax.dot_general(
        weight_nine, grad_rows[: 9 * local_ch], (((0,), (0,)), ((), ())),
        preferred_element_type=f32,
    ).reshape(n_xy, 2, local_ch, width)
    give = lax.dynamic_index_in_dim(partial, 1 - core, 1, keepdims=False)
    taken = lax.ppermute(give, "c", swap)
    keep = lax.dynamic_index_in_dim(partial, core, 1, keepdims=False)
    partial = (keep + taken).astype(bf16)
    by_xy, partial, weight_nine = lax.optimization_barrier((by_xy, partial, weight_nine))
    other = lax.ppermute(by_xy, "c", swap)
    mine = jnp.arange(2) == core
    gathered = jnp.where(mine[None, :, None, None], by_xy[:, None], other[:, None])
    gathered = gathered.reshape(all_ch, width)

    taps = lax.dot_general(
        grad_rows, gathered, (((1,), (1,)), ((), ())), preferred_element_type=f32
    )
    taps = taps.astype(bf16).reshape(n_z, chunk_rows, all_ch)
    by_z = lax.all_to_all(taps, "z", 0, 0, tiled=True)

    block_out = pl.pallas_call(forward_kernel, out_shape=tile, name="forward", compiler_params=SMALL)(
        weight_nine, gathered, inputs
    )
    at = lax.axis_index("x")
    by_chip = partial.reshape(n_x, 2, local_ch, width)
    pick = lambda k: lax.dynamic_index_in_dim(by_chip, lax.rem(at + k, n_x), 0, keepdims=False)
    moved = [
        lax.ppermute(pick(k), "x", [(i, (i + k) % n_x) for i in range(n_x)])
        for k in range(1, n_x)
    ]
    pair = sum((m.astype(f32) for m in moved), pick(0).astype(f32)).astype(bf16)
    row = lax.axis_index("yh")
    taken = lax.ppermute(
        lax.dynamic_index_in_dim(pair, 1 - row, 0, keepdims=False), "yh", swap
    )
    keep = lax.dynamic_index_in_dim(pair, row, 0, keepdims=False)
    input_grad = pl.pallas_call(back_kernel, out_shape=tile, name="back", compiler_params=SMALL)(
        keep, taken, normed, pre_act, inv, gain_row, out_grad
    )

    z_sum = pl.pallas_call(
        sum_copies_kernel,
        out_shape=jax.ShapeDtypeStruct((n_yl, chunk_rows, all_ch), f32),
        name="sum_z", compiler_params=SMALL,
    )(by_z)
    by_yl = lax.all_to_all(z_sum, "yl", 0, 0, tiled=True)
    first_old, second_old = BETA_ONE * moment_one, BETA_TWO * moment_two
    by_yl, first_old, second_old = lax.optimization_barrier((by_yl, first_old, second_old))
    total = (jnp.sum(by_yl, axis=0) / n_dp).astype(bf16)
    total = lax.all_gather(total, "z", axis=0, tiled=True)
    gradient = total[: 9 * local_ch].reshape(9, local_ch, all_ch).astype(f32)

    first_new = first_old + (1.0 - BETA_ONE) * gradient
    second_new = second_old + (1.0 - BETA_TWO) * gradient * gradient
    weight_new = conv_weight - LEARN_RATE * (first_new / CORRECT_ONE) / (
        jnp.sqrt(second_new / CORRECT_TWO) + EPS_ADAM
    )
    return (block_out, input_grad, weight_new, first_new, second_new)


def solution(mesh):
    five = Mesh(mesh.devices.reshape(12, 4, 4, 2, 2), ("z", "yl", "x", "yh", "c"))
    act, chan, wgt = P(FSDP, DP), P(FSDP), P(None, FSDP, None)
    return jax.shard_map(
        step,
        mesh=five,
        in_specs=(act, chan, chan, wgt, wgt, wgt, act),
        out_specs=(act, act, wgt, wgt, wgt),
        check_vma=False,
    )
```

```python
import jax
import jax.numpy as jnp
from jax import lax
from jax.experimental import pallas as pl
from jax.experimental.pallas import tpu as pltpu
from jax.sharding import Mesh, PartitionSpec as P

SIDE = 32

EPS_NORM = 1e-05
BETA_ONE = 0.9
BETA_TWO = 0.999
CORRECT_ONE = 1.0 - 0.9**10
CORRECT_TWO = 1.0 - 0.999**10
LEARN_RATE = 0.001
EPS_ADAM = 1e-08
OFFSETS = ((-1, -1), (-1, 0), (-1, 1), (0, -1), (0, 0), (0, 1), (1, -1), (1, 0), (1, 1))

SMALL = pltpu.CompilerParams(vmem_limit_bytes=16 * 2**20)
DP = ("z", "yl")
FSDP = ("x", "yh", "c")
XY = ("x", "yh")


def shifted(source, a, b):
    if a == 0 and b == 0:
        return source
    width = source.shape[-1]
    position = lax.broadcasted_iota(jnp.int32, (1, width), 1)
    row, col = position // SIDE, position % SIDE
    inside = (row + a >= 0) & (row + a < SIDE) & (col + b >= 0) & (col + b < SIDE)
    moved = pltpu.roll(source, (-(a * SIDE + b)) % width, 1)
    return jnp.where(inside, moved, 0.0)


def column(row):
    n = row.shape[1]
    eye = lax.broadcasted_iota(jnp.int32, (n, n), 0) == lax.broadcasted_iota(jnp.int32, (n, n), 1)
    return jnp.sum(jnp.where(eye, row, 0.0), axis=1, keepdims=True)


def norm_kernel(x_ref, gain_ref, bias_ref, act_ref, normed_ref, pre_ref, inv_ref):
    x = x_ref[...]
    count = x.shape[0] * x.shape[1]
    mean = jnp.sum(jnp.sum(x, axis=0, keepdims=True), axis=1, keepdims=True) / count
    centred = x - mean
    var = jnp.sum(jnp.sum(centred * centred, axis=0, keepdims=True), axis=1, keepdims=True) / count
    inv = lax.rsqrt(var + EPS_NORM)
    normed = centred * inv
    pre = normed * column(gain_ref[...]) + column(bias_ref[...])
    normed_ref[...] = normed
    pre_ref[...] = pre
    inv_ref[...] = jnp.broadcast_to(inv, inv_ref.shape)
    act = (pre * jax.nn.sigmoid(pre)).astype(jnp.bfloat16)
    for copy in range(act_ref.shape[0]):
        act_ref[copy] = act


def nine_kernel(g_ref, out_ref):
    g = g_ref[...].astype(jnp.bfloat16).astype(jnp.float32)
    rows = g.shape[0]
    for tap, (a, b) in enumerate(OFFSETS):
        out_ref[tap * rows : (tap + 1) * rows, :] = shifted(g, -a, -b).astype(jnp.bfloat16)
    rest = out_ref.shape[0] - 9 * rows
    out_ref[9 * rows :, :] = jnp.zeros((rest, g.shape[1]), jnp.bfloat16)


def forward_kernel(w_ref, act_ref, x_ref, out_ref):
    rows = x_ref.shape[0]
    products = jnp.dot(w_ref[...], act_ref[...], preferred_element_type=jnp.float32)
    total = x_ref[...]
    for tap, (a, b) in enumerate(OFFSETS):
        total = total + shifted(products[tap * rows : (tap + 1) * rows, :], a, b)
    out_ref[...] = total


def sum_copies_kernel(parts_ref, out_ref):
    total = jnp.sum(parts_ref[...].astype(jnp.float32), axis=0).astype(out_ref.dtype)
    for copy in range(out_ref.shape[0]):
        out_ref[copy] = total


def back_kernel(keep_ref, taken_ref, normed_ref, pre_ref, inv_ref, gain_ref, grad_ref, out_ref):
    grad_act = keep_ref[...].astype(jnp.float32) + taken_ref[...].astype(jnp.float32)
    pre, normed = pre_ref[...], normed_ref[...]
    s = jax.nn.sigmoid(pre)
    gn = grad_act * s * (1.0 + pre * (1.0 - s)) * column(gain_ref[...])
    count = gn.shape[0] * gn.shape[1]
    first = jnp.sum(jnp.sum(gn, axis=0, keepdims=True), axis=1, keepdims=True) / count
    second = jnp.sum(jnp.sum(gn * normed, axis=0, keepdims=True), axis=1, keepdims=True) / count
    out_ref[...] = grad_ref[...] + inv_ref[0:1, 0:1] * (gn - first - normed * second)


def step(inputs, norm_gain, norm_bias, conv_weight, moment_one, moment_two, out_grad):
    local_ch, width = inputs.shape
    n_fsdp = lax.axis_size(FSDP)
    n_z, n_yl, n_x = lax.axis_size("z"), lax.axis_size("yl"), lax.axis_size("x")
    n_dp, n_xy = n_z * n_yl, lax.axis_size(XY)
    all_ch = local_ch * n_fsdp
    f32, bf16 = jnp.float32, jnp.bfloat16
    chunk_rows = -(-(9 * local_ch) // (8 * n_z)) * 8
    pad_rows = chunk_rows * n_z
    swap = [(0, 1), (1, 0)]
    gain_row, bias_row = norm_gain[None, :], norm_bias[None, :]

    tile = jax.ShapeDtypeStruct((local_ch, width), f32)
    act, normed, pre_act, inv = pl.pallas_call(
        norm_kernel,
        out_shape=(
            jax.ShapeDtypeStruct((n_xy, local_ch, width), bf16), tile, tile,
            jax.ShapeDtypeStruct((8, 128), f32),
        ),
        name="norm",
    )(inputs, gain_row, bias_row)

    grad_rows = pl.pallas_call(
        nine_kernel, out_shape=jax.ShapeDtypeStruct((pad_rows, width), bf16), name="nine", compiler_params=SMALL
    )(out_grad)
    weight_nine = conv_weight.astype(bf16).reshape(9 * local_ch, all_ch)

    by_xy = lax.all_to_all(act, XY, 0, 0, tiled=True)
    core = lax.axis_index("c")
    partial = lax.dot_general(
        weight_nine, grad_rows[: 9 * local_ch], (((0,), (0,)), ((), ())),
        preferred_element_type=f32,
    ).reshape(n_xy, 2, local_ch, width)
    give = lax.dynamic_index_in_dim(partial, 1 - core, 1, keepdims=False)
    taken = lax.ppermute(give, "c", swap)
    keep = lax.dynamic_index_in_dim(partial, core, 1, keepdims=False)
    partial = (keep + taken).astype(bf16)
    by_xy, partial, weight_nine = lax.optimization_barrier((by_xy, partial, weight_nine))
    other = lax.ppermute(by_xy, "c", swap)
    mine = jnp.arange(2) == core
    gathered = jnp.where(mine[None, :, None, None], by_xy[:, None], other[:, None])
    gathered = gathered.reshape(all_ch, width)

    taps = lax.dot_general(
        grad_rows, gathered, (((1,), (1,)), ((), ())), preferred_element_type=f32
    )
    taps = taps.astype(bf16).reshape(n_z, chunk_rows, all_ch)
    by_z = lax.all_to_all(taps, "z", 0, 0, tiled=True)

    block_out = pl.pallas_call(forward_kernel, out_shape=tile, name="forward")(
        weight_nine, gathered, inputs
    )
    at = lax.axis_index("x")
    by_chip = partial.reshape(n_x, 2, local_ch, width)
    pick = lambda k: lax.dynamic_index_in_dim(by_chip, lax.rem(at + k, n_x), 0, keepdims=False)
    moved = [
        lax.ppermute(pick(k), "x", [(i, (i + k) % n_x) for i in range(n_x)])
        for k in range(1, n_x)
    ]
    pair = sum((m.astype(f32) for m in moved), pick(0).astype(f32)).astype(bf16)
    row = lax.axis_index("yh")
    taken = lax.ppermute(
        lax.dynamic_index_in_dim(pair, 1 - row, 0, keepdims=False), "yh", swap
    )
    keep = lax.dynamic_index_in_dim(pair, row, 0, keepdims=False)
    input_grad = pl.pallas_call(back_kernel, out_shape=tile, name="back")(
        keep, taken, normed, pre_act, inv, gain_row, out_grad
    )

    z_sum = pl.pallas_call(
        sum_copies_kernel,
        out_shape=jax.ShapeDtypeStruct((n_yl, chunk_rows, all_ch), f32),
        name="sum_z", compiler_params=SMALL,
    )(by_z)
    by_yl = lax.all_to_all(z_sum, "yl", 0, 0, tiled=True)
    total = (jnp.sum(by_yl, axis=0) / n_dp).astype(bf16)
    total = lax.all_gather(total, "z", axis=0, tiled=True)
    gradient = total[: 9 * local_ch].reshape(9, local_ch, all_ch).astype(f32)

    first_new = BETA_ONE * moment_one + (1.0 - BETA_ONE) * gradient
    second_new = BETA_TWO * moment_two + (1.0 - BETA_TWO) * gradient * gradient
    weight_new = conv_weight - LEARN_RATE * (first_new / CORRECT_ONE) / (
        jnp.sqrt(second_new / CORRECT_TWO) + EPS_ADAM
    )
    return (block_out, input_grad, weight_new, first_new, second_new)


def solution(mesh):
    five = Mesh(mesh.devices.reshape(12, 4, 4, 2, 2), ("z", "yl", "x", "yh", "c"))
    act, chan, wgt = P(FSDP, DP), P(FSDP), P(None, FSDP, None)
    return jax.shard_map(
        step,
        mesh=five,
        in_specs=(act, chan, chan, wgt, wgt, wgt, act),
        out_specs=(act, act, wgt, wgt, wgt),
        check_vma=False,
    )
```

```python
import jax
import jax.numpy as jnp
from jax import lax
from jax.experimental import pallas as pl
from jax.experimental.pallas import tpu as pltpu
from jax.sharding import Mesh, PartitionSpec as P

SIDE = 32

EPS_NORM = 1e-05
BETA_ONE = 0.9
BETA_TWO = 0.999
CORRECT_ONE = 1.0 - 0.9**10
CORRECT_TWO = 1.0 - 0.999**10
LEARN_RATE = 0.001
EPS_ADAM = 1e-08
OFFSETS = ((-1, -1), (-1, 0), (-1, 1), (0, -1), (0, 0), (0, 1), (1, -1), (1, 0), (1, 1))

SMALL = pltpu.CompilerParams(vmem_limit_bytes=16 * 2**20)
DP = ("z", "yl")
FSDP = ("x", "yh", "c")
XY = ("x", "yh")


def shifted(source, a, b):
    if a == 0 and b == 0:
        return source
    width = source.shape[-1]
    position = lax.broadcasted_iota(jnp.int32, (1, width), 1)
    row, col = position // SIDE, position % SIDE
    inside = (row + a >= 0) & (row + a < SIDE) & (col + b >= 0) & (col + b < SIDE)
    moved = pltpu.roll(source, (-(a * SIDE + b)) % width, 1)
    return jnp.where(inside, moved, 0.0)


def column(row):
    n = row.shape[1]
    eye = lax.broadcasted_iota(jnp.int32, (n, n), 0) == lax.broadcasted_iota(jnp.int32, (n, n), 1)
    return jnp.sum(jnp.where(eye, row, 0.0), axis=1, keepdims=True)


def norm_kernel(x_ref, gain_ref, bias_ref, act_ref, normed_ref, inv_ref):
    x = x_ref[...]
    count = x.shape[0] * x.shape[1]
    mean = jnp.sum(jnp.sum(x, axis=0, keepdims=True), axis=1, keepdims=True) / count
    centred = x - mean
    var = jnp.sum(jnp.sum(centred * centred, axis=0, keepdims=True), axis=1, keepdims=True) / count
    inv = lax.rsqrt(var + EPS_NORM)
    normed = centred * inv
    pre = normed * column(gain_ref[...]) + column(bias_ref[...])
    normed_ref[...] = normed
    inv_ref[...] = jnp.broadcast_to(inv, inv_ref.shape)
    act = (pre * jax.nn.sigmoid(pre)).astype(jnp.bfloat16)
    for copy in range(act_ref.shape[0]):
        act_ref[copy] = act


def nine_kernel(g_ref, out_ref):
    g = g_ref[...].astype(jnp.bfloat16).astype(jnp.float32)
    rows = g.shape[0]
    for tap, (a, b) in enumerate(OFFSETS):
        out_ref[tap * rows : (tap + 1) * rows, :] = shifted(g, -a, -b).astype(jnp.bfloat16)
    rest = out_ref.shape[0] - 9 * rows
    out_ref[9 * rows :, :] = jnp.zeros((rest, g.shape[1]), jnp.bfloat16)


def forward_kernel(w_ref, act_ref, x_ref, out_ref):
    rows = x_ref.shape[0]
    products = jnp.dot(w_ref[...], act_ref[...], preferred_element_type=jnp.float32)
    total = x_ref[...]
    for tap, (a, b) in enumerate(OFFSETS):
        total = total + shifted(products[tap * rows : (tap + 1) * rows, :], a, b)
    out_ref[...] = total


def sum_copies_kernel(parts_ref, out_ref):
    total = jnp.sum(parts_ref[...].astype(jnp.float32), axis=0).astype(out_ref.dtype)
    for copy in range(out_ref.shape[0]):
        out_ref[copy] = total


def back_kernel(keep_ref, taken_ref, normed_ref, inv_ref, gain_ref, bias_ref, grad_ref, out_ref):
    grad_act = keep_ref[...].astype(jnp.float32) + taken_ref[...].astype(jnp.float32)
    normed, gain = normed_ref[...], column(gain_ref[...])
    pre = normed * gain + column(bias_ref[...])
    s = jax.nn.sigmoid(pre)
    gn = grad_act * s * (1.0 + pre * (1.0 - s)) * gain
    count = gn.shape[0] * gn.shape[1]
    first = jnp.sum(jnp.sum(gn, axis=0, keepdims=True), axis=1, keepdims=True) / count
    second = jnp.sum(jnp.sum(gn * normed, axis=0, keepdims=True), axis=1, keepdims=True) / count
    out_ref[...] = grad_ref[...] + inv_ref[0:1, 0:1] * (gn - first - normed * second)


def step(inputs, norm_gain, norm_bias, conv_weight, moment_one, moment_two, out_grad):
    local_ch, width = inputs.shape
    n_fsdp = lax.axis_size(FSDP)
    n_z, n_yl, n_x = lax.axis_size("z"), lax.axis_size("yl"), lax.axis_size("x")
    n_dp, n_xy = n_z * n_yl, lax.axis_size(XY)
    all_ch = local_ch * n_fsdp
    f32, bf16 = jnp.float32, jnp.bfloat16
    chunk_rows = -(-(9 * local_ch) // (8 * n_z)) * 8
    pad_rows = chunk_rows * n_z
    swap = [(0, 1), (1, 0)]
    gain_row, bias_row = norm_gain[None, :], norm_bias[None, :]

    tile = jax.ShapeDtypeStruct((local_ch, width), f32)
    act, normed, inv = pl.pallas_call(
        norm_kernel,
        out_shape=(
            jax.ShapeDtypeStruct((n_xy, local_ch, width), bf16), tile,
            jax.ShapeDtypeStruct((8, 128), f32),
        ),
        name="norm",
    )(inputs, gain_row, bias_row)

    grad_rows = pl.pallas_call(
        nine_kernel, out_shape=jax.ShapeDtypeStruct((pad_rows, width), bf16), name="nine", compiler_params=SMALL
    )(out_grad)
    weight_nine = conv_weight.astype(bf16).reshape(9 * local_ch, all_ch)

    by_xy = lax.all_to_all(act, XY, 0, 0, tiled=True)
    core = lax.axis_index("c")
    partial = lax.dot_general(
        weight_nine, grad_rows[: 9 * local_ch], (((0,), (0,)), ((), ())),
        preferred_element_type=f32,
    ).reshape(n_xy, 2, local_ch, width)
    give = lax.dynamic_index_in_dim(partial, 1 - core, 1, keepdims=False)
    taken = lax.ppermute(give, "c", swap)
    keep = lax.dynamic_index_in_dim(partial, core, 1, keepdims=False)
    partial = (keep + taken).astype(bf16)
    by_xy, partial, weight_nine = lax.optimization_barrier((by_xy, partial, weight_nine))
    other = lax.ppermute(by_xy, "c", swap)
    mine = jnp.arange(2) == core
    gathered = jnp.where(mine[None, :, None, None], by_xy[:, None], other[:, None])
    gathered = gathered.reshape(all_ch, width)

    taps = lax.dot_general(
        grad_rows, gathered, (((1,), (1,)), ((), ())), preferred_element_type=f32
    )
    taps = taps.astype(bf16).reshape(n_z, chunk_rows, all_ch)
    by_z = lax.all_to_all(taps, "z", 0, 0, tiled=True)

    block_out = pl.pallas_call(forward_kernel, out_shape=tile, name="forward")(
        weight_nine, gathered, inputs
    )
    at = lax.axis_index("x")
    by_chip = partial.reshape(n_x, 2, local_ch, width)
    pick = lambda k: lax.dynamic_index_in_dim(by_chip, lax.rem(at + k, n_x), 0, keepdims=False)
    moved = [
        lax.ppermute(pick(k), "x", [(i, (i + k) % n_x) for i in range(n_x)])
        for k in range(1, n_x)
    ]
    pair = sum((m.astype(f32) for m in moved), pick(0).astype(f32)).astype(bf16)
    row = lax.axis_index("yh")
    taken = lax.ppermute(
        lax.dynamic_index_in_dim(pair, 1 - row, 0, keepdims=False), "yh", swap
    )
    keep = lax.dynamic_index_in_dim(pair, row, 0, keepdims=False)
    input_grad = pl.pallas_call(back_kernel, out_shape=tile, name="back")(
        keep, taken, normed, inv, gain_row, bias_row, out_grad
    )

    z_sum = pl.pallas_call(
        sum_copies_kernel,
        out_shape=jax.ShapeDtypeStruct((n_yl, chunk_rows, all_ch), f32),
        name="sum_z", compiler_params=SMALL,
    )(by_z)
    by_yl = lax.all_to_all(z_sum, "yl", 0, 0, tiled=True)
    total = (jnp.sum(by_yl, axis=0) / n_dp).astype(bf16)
    total = lax.all_gather(total, "z", axis=0, tiled=True)
    gradient = total[: 9 * local_ch].reshape(9, local_ch, all_ch).astype(f32)

    first_new = BETA_ONE * moment_one + (1.0 - BETA_ONE) * gradient
    second_new = BETA_TWO * moment_two + (1.0 - BETA_TWO) * gradient * gradient
    weight_new = conv_weight - LEARN_RATE * (first_new / CORRECT_ONE) / (
        jnp.sqrt(second_new / CORRECT_TWO) + EPS_ADAM
    )
    return (block_out, input_grad, weight_new, first_new, second_new)


def solution(mesh):
    five = Mesh(mesh.devices.reshape(12, 4, 4, 2, 2), ("z", "yl", "x", "yh", "c"))
    act, chan, wgt = P(FSDP, DP), P(FSDP), P(None, FSDP, None)
    return jax.shard_map(
        step,
        mesh=five,
        in_specs=(act, chan, chan, wgt, wgt, wgt, act),
        out_specs=(act, act, wgt, wgt, wgt),
        check_vma=False,
    )
```
